32 devices in a mesh: wall: 8 (over y, x, core), span: 4 (over z).
Axes of the slice: x: 2, y: 2, z: 4, core: 2. Of those that a mesh axis runs over, the one named last changes fastest.
Arguments:
- velocity_old: float32 [3, 128, 64, 128], P(None, 'wall', 'span'), may hold values from -12 to 12, as said below
- heights: float32 [16], replicated, may hold values from 0.04 to 0.25
- owner_device: int32 [16384, 1], P(('wall', 'span')), may hold values from 0 to 7, as said below
- owner_element: int32 [16384, 1], P(('wall', 'span')), may hold values from 0 to 63, as said below
- ref_coords: float32 [3, 16384], P(None, ('wall', 'span')), may hold values from -1 to 1
- roughness: float32 [16384], P(('wall', 'span')), may hold values from 0.0001 to 0.01
Outputs:
- velocity_new: float32 [3, 128, 64, 128], P(None, 'wall', 'span')
- neumann: float32 [2, 16384], P(None, ('wall', 'span'))
The draws below stay inside these ranges and needn't reach their ends.
Inputs may be any that keep to these rules, and one draw needn't show every extreme that they name: `velocity_old`: values at coinciding nodes of neighbouring elements are equal. `owner_device`: the owner is the streamwise index w of the point's own device, or w + 1 or w - 1 modulo 8. Among the rows of one device at most 128 name w + 1 and at most 128 name w - 1; some device has exactly 128 for w + 1 and some device exactly 128 for w - 1. `owner_element`: the element index is (ex * 2 + ez) * 16 + ey with ex = i // 8 and ez = j // 8 of the wall point; ey < 2 for points of the first wall, ey >= 14 for the second.
All inputs are finite; a program needn't handle non-finite values.
Results may differ from the reference program's by a relative error of at most 0.0003.
Values sent between devices are 32-bit elements; how exact they have to be, the bound alone decides.
No kernel may reach another device: no remote copies, remote signals or barrier semaphores. Data moves between devices by JAX's collectives and lax.ppermute only.
A program may use at most 128 MiB of HBM per device.

```python
import math
import jax
import jax.numpy as jnp
import numpy as np
from jax import lax

ORDER = 7
QN = 8
EXD = 2
EZD = 2
EY = 16
NEAR = 2
ITERS = 3
XLOC = 16
ZLOC = 16
YNODES = 128
XNODES = 128
ZNODES = 64
P_DEV = 512
WALLPTS = 16384
CAP = 128
N_WALL = 8
N_SPAN = 4
DEVICES = 32


def draw_velocity_old(key, part):
    unique_x = XNODES // QN * ORDER
    unique_z = ZNODES // QN * ORDER
    unique_y = EY * ORDER + 1
    index_x = (jnp.arange(XNODES) // QN * ORDER + jnp.arange(XNODES) % QN) % unique_x
    index_z = (jnp.arange(ZNODES) // QN * ORDER + jnp.arange(ZNODES) % QN) % unique_z
    index_y = jnp.arange(YNODES) // QN * ORDER + jnp.arange(YNODES) % QN
    shape_grid = (3, unique_x, unique_z, unique_y)
    values_grid = jax.random.truncated_normal(key, -4.0, 4.0, shape_grid, jnp.float32)
    rising = jnp.exp(jnp.log(3.0) * jnp.arange(unique_x, dtype=jnp.float32) / unique_x)
    values_grid = values_grid * rising[None, :, None, None]
    values_grid = jnp.take(values_grid, index_x, axis=1)
    values_grid = jnp.take(values_grid, index_z, axis=2)
    return jnp.take(values_grid, index_y, axis=3)


def draw_owner_device(key, part):
    block_keys = jax.random.split(jax.random.fold_in(key, 21), DEVICES)
    ranks = jax.vmap(lambda single: jax.random.permutation(single, P_DEV))(block_keys).astype(jnp.int32)
    blocks = jnp.arange(DEVICES, dtype=jnp.int32)
    count_next = jax.random.randint(jax.random.fold_in(key, 22), (DEVICES,), CAP // 3, CAP + 1)
    count_prev = jax.random.randint(jax.random.fold_in(key, 23), (DEVICES,), CAP // 3, CAP + 1)
    full_next = jax.random.randint(jax.random.fold_in(key, 24), (), 0, DEVICES)
    full_prev = jax.random.randint(jax.random.fold_in(key, 25), (), 0, DEVICES)
    count_next = jnp.where(blocks == full_next, CAP, count_next)
    count_prev = jnp.where(blocks == full_prev, CAP, count_prev)
    offset = jnp.where(ranks < count_next[:, None], 1, jnp.where(ranks < (count_next + count_prev)[:, None], -1, 0))
    own_wall = (blocks // N_SPAN)[:, None]
    owner = (own_wall + offset + N_WALL) % N_WALL
    return owner.astype(jnp.int32).reshape(WALLPTS, 1)


def draw_owner_element(key, part):
    position = jnp.arange(WALLPTS, dtype=jnp.int32) % P_DEV
    side_flag = position // (P_DEV // 2)
    node_i = position // ZLOC % XLOC
    node_j = position % ZLOC
    elem_x = node_i // QN
    elem_z = node_j // QN
    layer = jax.random.randint(jax.random.fold_in(key, 13), (WALLPTS,), 0, NEAR)
    elem_y = jnp.where(side_flag == 1, EY - 1 - layer, layer)
    return ((elem_x * EZD + elem_z) * EY + elem_y).astype(jnp.int32).reshape(WALLPTS, 1)


def levels(rng, shape, cuts, low, high):
    level = 1.0
    for axis_at, parts in cuts:
        steps = jax.random.uniform(jax.random.fold_in(jax.random.fold_in(rng, 6), axis_at), (parts,), jnp.float32, low / len(cuts), high / len(cuts))
        level = level * jnp.repeat(jnp.exp(steps), shape[axis_at] // parts).reshape((-1,) + (1,) * (len(shape) - 1 - axis_at))
    return level


def setup_inputs(seed: int = 0) -> dict:
    keys = jax.random.split(jax.random.key(seed), 7)
    return {
        "velocity_old": draw_velocity_old(jax.random.fold_in(keys[6], 71), 0),
        "heights": jnp.clip(jnp.exp(jax.random.uniform(keys[1], (EY,), jnp.float32, math.log(0.04), math.log(0.25))), 0.04, 0.25),
        "owner_device": draw_owner_device(jax.random.fold_in(keys[6], 71), 0),
        "owner_element": draw_owner_element(jax.random.fold_in(keys[6], 71), 0),
        "ref_coords": jnp.clip(jax.random.uniform(keys[4], (3, WALLPTS), jnp.float32, -1.0, 1.0) * levels(keys[4], (3, WALLPTS), ((1, 32),), -0.4, 0.0), -1.0, 1.0),
        "roughness": jnp.clip(jnp.exp(math.log(0.01) - 4.6051702 * jax.random.uniform(keys[5], (WALLPTS,), jnp.float32) ** levels(keys[5], (WALLPTS,), ((0, 32),), -0.2, 0.2)), 0.0001, 0.01),
    }


GLL_NODES = (-1.0, -0.8717401485096066, -0.5917001814331423, -0.2092992179024789, 0.2092992179024789, 0.5917001814331423, 0.8717401485096066, 1.0)
GLL_WEIGHTS = (0.03571428571428571, 0.2107042271435061, 0.3411226924835044, 0.4124587946587038, 0.4124587946587038, 0.3411226924835044, 0.2107042271435061, 0.03571428571428571)
viscosity = 0.02
inverse_step = 20.0
karman = 0.41
sample_height = 0.1
speed_floor = 0.01
element_dx = 0.05
element_dz = 0.13
precise = lax.Precision.HIGHEST

def stiffness_table():
    points = np.array(GLL_NODES)
    weights = np.array(GLL_WEIGHTS)
    previous = np.ones(8)
    current = points.copy()
    for degree in range(1, 7):
        previous, current = (current, ((2 * degree + 1) * points * current - degree * previous) / (degree + 1))
    derivative = np.zeros((8, 8))
    for target in range(8):
        for source in range(8):
            if target != source:
                derivative[target, source] = current[target] / current[source] / (points[target] - points[source])
    derivative[0, 0] = -14.0
    derivative[7, 7] = 14.0
    return derivative.T @ (weights[:, None] * derivative)

def lagrange(coord):
    points = np.array(GLL_NODES)
    gaps_table = points[:, None] - points[None, :] + np.eye(8)
    scale_row = jnp.asarray(1.0 / np.prod(gaps_table, axis=1), jnp.float32)
    gaps = coord[:, None] - jnp.asarray(points, jnp.float32)[None, :]
    filled = jnp.where(jnp.asarray(np.eye(8) > 0.5)[None], jnp.float32(1.0), gaps[:, None, :])
    return jnp.prod(filled, axis=2) * scale_row[None, :]

def face_weights(length, open_ends):
    values = np.ones(length)
    position = np.arange(length) % 8
    values[(position == 0) | (position == 7)] = 0.5
    if open_ends:
        values[0] = 1.0
        values[-1] = 1.0
    return values

def join_faces(core, before, after, axis):
    count = core.shape[axis] // 8
    blocks = core.reshape(core.shape[:axis] + (count, 8) + core.shape[axis + 1:])
    first = lax.slice_in_dim(blocks, 0, 1, axis=axis + 1)
    last = lax.slice_in_dim(blocks, 7, 8, axis=axis + 1)
    before_b = jnp.expand_dims(before, axis + 1)
    after_b = jnp.expand_dims(after, axis + 1)
    prev_last = jnp.concatenate([before_b, lax.slice_in_dim(last, 0, count - 1, axis=axis)], axis)
    next_first = jnp.concatenate([lax.slice_in_dim(first, 1, count, axis=axis), after_b], axis)
    middle = lax.slice_in_dim(blocks, 1, 7, axis=axis + 1)
    joined = jnp.concatenate([first + prev_last, middle, last + next_first], axis + 1)
    return joined.reshape(core.shape)

def assemble(field):
    joined_x = join_faces(field, field[:, -1:], field[:, :1], 1)
    joined_z = join_faces(joined_x, joined_x[:, :, -1:], joined_x[:, :, :1], 2)
    border = jnp.zeros(joined_z.shape[:3] + (1,), jnp.float32)
    return join_faces(joined_z, border, border, 3)

def reference(velocity_old, heights, owner_device, owner_element, ref_coords, roughness):
    weights = np.array(GLL_WEIGHTS)
    stiffness = jnp.asarray(stiffness_table(), jnp.float32)
    length_x, length_z, length_y = (velocity_old.shape[1], velocity_old.shape[2], velocity_old.shape[3])
    count_x, count_z, count_y = (length_x // 8, length_z // 8, length_y // 8)
    mass_x = jnp.asarray(np.tile(0.5 * element_dx * weights, count_x), jnp.float32)
    mass_z = jnp.asarray(np.tile(0.5 * element_dz * weights, count_z), jnp.float32)
    mass_y = (0.5 * heights[:, None] * jnp.asarray(weights, jnp.float32)[None, :]).reshape(length_y)
    mass_all = mass_x[:, None, None] * mass_z[None, :, None] * mass_y[None, None, :]
    inverse_count = jnp.asarray(face_weights(length_x, False)[:, None, None] * face_weights(length_z, False)[None, :, None] * face_weights(length_y, True)[None, None, :], jnp.float32)
    blocks = (2.0 / heights)[:, None, None] * stiffness[None]

    def operate(field):
        along_x = jnp.einsum('ab,cebzy->ceazy', stiffness * (2.0 / element_dx), field.reshape(3, count_x, 8, length_z, length_y), precision=precise).reshape(field.shape)
        along_z = jnp.einsum('ab,cxeby->cxeay', stiffness * (2.0 / element_dz), field.reshape(3, length_x, count_z, 8, length_y), precision=precise).reshape(field.shape)
        along_y = jnp.einsum('eab,cxzeb->cxzea', blocks, field.reshape(3, length_x, length_z, count_y, 8), precision=precise).reshape(field.shape)
        mass_xb = mass_x[None, :, None, None]
        mass_zb = mass_z[None, None, :, None]
        mass_yb = mass_y[None, None, None, :]
        local = viscosity * (along_x * mass_zb * mass_yb + mass_xb * along_z * mass_yb + mass_xb * mass_zb * along_y) + inverse_step * mass_all[None] * field
        return assemble(local)
    element_rows = velocity_old.reshape(3, count_x, 8, count_z, 8, count_y, 8).transpose(1, 3, 5, 0, 2, 4, 6).reshape(count_x * count_z * count_y, 3 * 512)
    points = jnp.arange(WALLPTS, dtype=jnp.int32)
    span_index = points // P_DEV % N_SPAN
    local_elem = owner_element[:, 0]
    elem_x = owner_device[:, 0] * EXD + local_elem // (EZD * EY)
    elem_z = span_index * EZD + local_elem // EY % EZD
    elem_y = local_elem % EY
    row_ids = ((elem_x * count_z + elem_z) * count_y + elem_y).astype(jnp.int32)

    def evaluate(pieces):
        rows_here, coords = pieces
        values = element_rows[rows_here].reshape(rows_here.shape[0], 3, 8, 8, 8)
        return jnp.einsum('gcabd,ga,gb,gd->gc', values, lagrange(coords[:, 0]), lagrange(coords[:, 1]), lagrange(coords[:, 2]), precision=precise)
    sampled = lax.map(evaluate, (row_ids.reshape(DEVICES, P_DEV), ref_coords.T.reshape(DEVICES, P_DEV, 3))).reshape(WALLPTS, 3)
    stream = sampled[:, 0]
    spanwise = sampled[:, 2]
    wall_speed = jnp.sqrt(stream * stream + spanwise * spanwise + speed_floor)
    drag_coeff = (karman / jnp.log(sample_height / roughness)) ** 2
    neumann = -(drag_coeff * wall_speed / viscosity)[None, :] * jnp.stack([stream, spanwise])
    traction = (viscosity * neumann).reshape(2, N_WALL, N_SPAN, 2, XLOC, ZLOC).transpose(0, 3, 1, 4, 2, 5).reshape(2, 2, length_x, length_z)
    traction = traction * (mass_x[:, None] * mass_z[None, :])[None, None]
    zero_plane = jnp.zeros((1, length_x, length_z), jnp.float32)
    bottom = jnp.concatenate([traction[0:1, 0], zero_plane, traction[1:2, 0]], axis=0)
    top_wall = jnp.concatenate([traction[0:1, 1], zero_plane, traction[1:2, 1]], axis=0)
    forcing = inverse_step * mass_all[None] * velocity_old
    forcing = forcing.at[:, :, :, 0].add(bottom).at[:, :, :, -1].add(top_wall)
    right_side = assemble(forcing)

    def weighted(first, second):
        return lax.optimization_barrier(jnp.sum(first * second * inverse_count[None], axis=(1, 2, 3)))

    def spread(values):
        return values[:, None, None, None]
    solution = jnp.zeros_like(right_side)
    residual = right_side
    direction = residual
    norm_now = weighted(residual, residual)
    for sweep in range(ITERS):
        applied = operate(direction)
        step_size = norm_now / weighted(direction, applied)
        solution = solution + spread(step_size) * direction
        residual = residual - spread(step_size) * applied
        norm_next = weighted(residual, residual)
        direction = residual + spread(norm_next / norm_now) * direction
        norm_now = norm_next
    return (solution, neumann)
```

```python
import jax
import jax.numpy as jnp
import numpy as np
from jax import lax
from jax.experimental import pallas as pl
from jax.experimental.pallas import tpu as pltpu
from jax.sharding import PartitionSpec as P

NEAR = 2


GLL_NODES = (
    -1.0,
    -0.8717401485096066,
    -0.5917001814331423,
    -0.2092992179024789,
    0.2092992179024789,
    0.5917001814331423,
    0.8717401485096066,
    1.0,
)
GLL_WEIGHTS = (
    0.03571428571428571,
    0.2107042271435061,
    0.3411226924835044,
    0.4124587946587038,
    0.4124587946587038,
    0.3411226924835044,
    0.2107042271435061,
    0.03571428571428571,
)
viscosity = 0.02
inverse_step = 20.0
karman = 0.41
sample_height = 0.1
speed_floor = 0.01
element_dx = 0.05
element_dz = 0.13
precise = lax.Precision.HIGHEST


def shifted(value, axis, steps):
    count = lax.axis_size(axis)
    pairs = [(source, (source + steps) % count) for source in range(count)]
    return lax.ppermute(value, axis, pairs)


def stiffness_table():
    points = np.array(GLL_NODES)
    weights = np.array(GLL_WEIGHTS)
    previous = np.ones(8)
    current = points.copy()
    for degree in range(1, 7):
        previous, current = (
            current,
            ((2 * degree + 1) * points * current - degree * previous) / (degree + 1),
        )
    derivative = np.zeros((8, 8))
    for target in range(8):
        for source in range(8):
            if target != source:
                derivative[target, source] = (
                    current[target] / current[source] / (points[target] - points[source])
                )
    derivative[0, 0] = -14.0
    derivative[7, 7] = 14.0
    return derivative.T @ (weights[:, None] * derivative)


def face_weights(length, open_ends):
    values = np.ones(length)
    position = np.arange(length) % 8
    values[(position == 0) | (position == 7)] = 0.5
    if open_ends:
        values[0] = 1.0
        values[-1] = 1.0
    return values


def join_matrix(length):
    table = np.eye(length)
    for node in range(7, length - 1, 8):
        table[node, node + 1] = 1.0
        table[node + 1, node] = 1.0
    return table


def exchange(x_low, x_high, z_low, z_high):
    from_prev = shifted(x_high, "wall", 1)
    from_next = shifted(x_low, "wall", -1)

    def with_corners(face, spot):
        first = face[:, :1] + from_prev[:, spot]
        last = face[:, -1:] + from_next[:, spot]
        return jnp.concatenate([first, face[:, 1:-1], last], axis=1)

    z_low = with_corners(z_low, slice(0, 1))
    z_high = with_corners(z_high, slice(-1, None))
    return from_prev, from_next, shifted(z_high, "span", 1), shifted(z_low, "span", -1)


def call(kernel, outs, *operands):
    space = pl.BlockSpec(memory_space=pltpu.VMEM)
    return pl.pallas_call(
        kernel,
        out_shape=[jax.ShapeDtypeStruct(shape, jnp.float32) for shape in outs],
        in_specs=[space] * len(operands),
        out_specs=[space] * len(outs),
    )(*operands)


def dot(first, second):
    return jnp.dot(first, second, precision=precise, preferred_element_type=jnp.float32)


def body(velocity_old, heights, owner_device, owner_element, ref_coords, roughness):
    weights = np.array(GLL_WEIGHTS)
    points = np.array(GLL_NODES)
    stiffness = stiffness_table()
    _, length_x, length_z, length_y = velocity_old.shape
    count_x, count_z, count_y = (length_x // 8, length_z // 8, length_y // 8)
    plane = length_x * length_z
    point_total = owner_device.shape[0]
    near = NEAR * 8

    mass_x = np.tile(0.5 * element_dx * weights, count_x)
    mass_z = np.tile(0.5 * element_dz * weights, count_z)
    stiff_x = np.kron(np.eye(count_x), stiffness * (2.0 / element_dx))
    stiff_z = np.kron(np.eye(count_z), stiffness * (2.0 / element_dz))
    join_x, join_z, join_y = (join_matrix(n) for n in (length_x, length_z, length_y))
    join_xz = np.kron(join_x, join_z)
    mass_xz = np.kron(mass_x, mass_z)
    plane_op = viscosity * (
        np.kron(stiff_x, np.diag(mass_z)) + np.kron(np.diag(mass_x), stiff_z)
    )
    left = jnp.asarray(
        np.concatenate([join_xz @ np.diag(mass_xz), join_xz @ plane_op], axis=1), jnp.float32
    )
    tiled = np.tile(weights, count_y)
    stiff_part = np.concatenate(
        [
            2.0 * viscosity * np.kron(np.eye(count_y), stiffness) @ join_y,
            np.zeros((length_y, length_y)),
        ],
        axis=1,
    ).reshape(count_y, 8, 2 * length_y)
    mass_part = np.concatenate(
        [inverse_step * 0.5 * tiled[:, None] * join_y, 0.5 * tiled[:, None] * join_y], axis=1
    ).reshape(count_y, 8, 2 * length_y)
    tall = heights[:, None, None]
    right = (
        jnp.asarray(stiff_part, jnp.float32) / tall + jnp.asarray(mass_part, jnp.float32) * tall
    ).reshape(length_y, 2 * length_y)

    def edge_sum(values):
        position = np.arange(values.shape[0]) % 8
        return np.where((position == 0) | (position == 7), 2.0 * values, values)

    columns = np.zeros((plane, 8))
    columns[:, 0] = np.kron(face_weights(length_x, False), face_weights(length_z, False))
    columns[:, 1] = np.kron(face_weights(length_x, True), face_weights(length_z, True))
    columns[:, 2] = inverse_step * np.kron(edge_sum(mass_x), edge_sum(mass_z))
    columns = jnp.asarray(columns, jnp.float32)
    share_y = jnp.asarray(face_weights(length_y, True)[None, :], jnp.float32)

    def packed_near():
        pieces = []
        for ex in range(count_x):
            for comp in (0, 2):
                block = velocity_old[comp, ex * 8 : ex * 8 + 8]
                pieces.append(block[:, :, :near])
                pieces.append(block[:, :, length_y - near :])
        return jnp.concatenate(pieces, axis=2).reshape(8 * length_z, count_x * 4 * near)

    own_near = packed_near()
    prev_near = shifted(own_near, "wall", 1)
    next_near = shifted(own_near, "wall", -1)
    wall_count = lax.axis_size("wall")
    own_wall = lax.axis_index("wall")
    distance = ((owner_device[:, 0] - own_wall + wall_count) % wall_count)[None, :]
    relation = jnp.where(distance == 1, 1.0, jnp.where(distance == 0, 0.0, -1.0))
    layer = (owner_element[:, 0] % count_y)[None, :]
    layer = jnp.where(layer < NEAR, layer, layer - (count_y - NEAR)).astype(jnp.float32)
    per_point = jnp.concatenate([ref_coords, relation, layer, roughness[None, :]], axis=0)
    lanes = count_x * 4 * near
    scale = 1.0 / np.prod(points[:, None] - points[None, :] + np.eye(8), axis=1)
    mass_row = jnp.asarray(mass_xz[None, :], jnp.float32)
    pick_z = np.zeros((plane, 2 * length_x))
    for x in range(length_x):
        pick_z[x * length_z, x] = 1.0
        pick_z[x * length_z + length_z - 1, length_x + x] = 1.0
    pick_z = jnp.asarray(pick_z, jnp.float32)
    join_const = jnp.asarray(join_xz, jnp.float32)

    def sample_kernel(own, prev, nxt, info, mass, join, pick, neu, trac, xl, xh, zl, zh):
        def basis(row):
            coord = info[row : row + 1, :]
            gaps = [coord - np.float32(p) for p in points]
            rows = []
            for a in range(8):
                value = None
                for b in range(8):
                    if b != a:
                        value = gaps[b] if value is None else value * gaps[b]
                rows.append(value * np.float32(scale[a]))
            return jnp.concatenate(rows, axis=0)

        along_x, along_z, along_y = basis(0), basis(1), basis(2)
        relation_row, layer_row = info[3:4, :], info[4:5, :]
        near_y = jnp.concatenate(
            [jnp.where(layer_row == np.float32(e), along_y, 0.0) for e in range(NEAR)], axis=0
        )
        full_y = jnp.concatenate([near_y] * (lanes // near), axis=0)
        row = lax.broadcasted_iota(jnp.int32, (lanes, point_total), 0)
        col = lax.broadcasted_iota(jnp.int32, (lanes, point_total), 1)
        fits = (row // (4 * near) == col % plane // (8 * length_z)) & (
            row // near % 2 == col // plane
        )
        comp = row // (2 * near) % 2
        zrow = lax.broadcasted_iota(jnp.int32, (8 * length_z, point_total), 0)
        zcol = lax.broadcasted_iota(jnp.int32, (8 * length_z, point_total), 1)
        tall_z = jnp.concatenate([along_z] * (count_z * 8), axis=0)
        tall_x = jnp.concatenate(
            [jnp.broadcast_to(along_x[a : a + 1, :], (length_z, point_total)) for a in range(8)],
            axis=0,
        )
        mix = jnp.where(zrow % length_z // 8 == zcol % length_z // 8, tall_z * tall_x, 0.0)
        sampled = []
        for k in range(2):
            table = jnp.where(fits & (comp == k), full_y, 0.0)
            picked = jnp.where(
                relation_row == 0.0,
                dot(own[...], table),
                jnp.where(relation_row > 0.0, dot(nxt[...], table), dot(prev[...], table)),
            )
            sampled.append(jnp.sum(picked * mix, axis=0, keepdims=True))
        stream, spanwise = sampled
        speed = jnp.sqrt(stream * stream + spanwise * spanwise + speed_floor)
        ratio = karman / jnp.log(sample_height / info[5:6, :])
        factor = -(ratio * ratio * speed / viscosity)
        neu[0:1, :] = factor * stream
        neu[1:2, :] = factor * spanwise
        half = []
        for value in (stream, spanwise):
            for side in range(2):
                part = (viscosity * (factor * value))[:, side * plane : (side + 1) * plane]
                half.append(part * mass[...])
        stacked = jnp.concatenate(half, axis=0)
        joined = dot(stacked, join[...])
        trac[...] = joined
        xl[...] = joined[:, :length_z]
        xh[...] = joined[:, plane - length_z :]
        picked_z = dot(joined, pick[...])
        zl[...] = picked_z[:, :length_x]
        zh[...] = picked_z[:, length_x:]

    neumann, traction, *edges = call(
        sample_kernel,
        [(2, point_total), (4, plane), (4, length_z), (4, length_z), (4, length_x), (4, length_x)],
        own_near, prev_near, next_near, per_point, mass_row, join_const, pick_z,
    )
    around = exchange(*edges)

    shape = (3, length_x, length_z, length_y)
    x_face, z_face = (3, length_z, length_y), (3, length_x, length_y)
    outs = [shape, shape, x_face, x_face, z_face, z_face, (8, length_y)]

    def apply(comp, field, left_ref, right_ref, cols, share, sums):
        both = dot(field, right_ref[...])
        stacked = jnp.concatenate([both[:, :length_y], both[:, length_y:]], axis=0)
        applied = dot(left_ref[...], stacked)
        sums[comp : comp + 1, :] = share[...] * jnp.sum(
            field * field * cols[:, 0:1], axis=0, keepdims=True
        )
        sums[comp + 3 : comp + 4, :] = share[...] * jnp.sum(
            field * applied * cols[:, 1:2], axis=0, keepdims=True
        )
        return applied

    def store(comp, field, applied, u, t, xl, xh, zl, zh):
        u[comp] = field.reshape(length_x, length_z, length_y)
        cube = applied.reshape(length_x, length_z, length_y)
        t[comp] = cube
        xl[comp] = cube[0]
        xh[comp] = cube[length_x - 1]
        zl[comp] = cube[:, 0, :]
        zh[comp] = cube[:, length_z - 1, :]

    spread_pick = np.zeros((2 * length_z + 2 * length_x, plane))
    for z in range(length_z):
        spread_pick[z, z] = 1.0
        spread_pick[length_z + z, plane - length_z + z] = 1.0
    for x in range(length_x):
        spread_pick[2 * length_z + x, x * length_z] = 1.0
        spread_pick[2 * length_z + length_x + x, x * length_z + length_z - 1] = 1.0
    spread_pick = jnp.asarray(spread_pick, jnp.float32)

    def first_kernel(
        v, trac, xp, xn, zp, zn, place, left_ref, right_ref, cols, share,
        u, t, xl, xh, zl, zh, sums,
    ):
        edge = jnp.concatenate([xp[...], xn[...], zp[...], zn[...]], axis=1)
        wall = trac[...] + dot(edge, place[...])
        wall = jnp.concatenate([wall, jnp.zeros((4, plane), jnp.float32)], axis=0)
        wall = jnp.transpose(wall)
        lane = lax.broadcasted_iota(jnp.int32, (plane, length_y), 1)
        tall_y = jnp.sum(right_ref[:, length_y:], axis=0, keepdims=True)
        sums[...] = jnp.zeros((8, length_y), jnp.float32)
        for comp in range(3):
            field = v[comp].reshape(plane, length_y) * (cols[:, 2:3] * tall_y)
            if comp != 1:
                at = comp
                field = field + jnp.where(lane == 0, wall[:, at : at + 1], 0.0)
                field = field + jnp.where(
                    lane == length_y - 1, wall[:, at + 1 : at + 2], 0.0
                )
            applied = apply(comp, field, left_ref, right_ref, cols, share, sums)
            store(comp, field, applied, u, t, xl, xh, zl, zh)

    def add_faces(comp, t_in, xp, xn, zp, zn):
        cube = t_in[comp]
        ix = lax.broadcasted_iota(jnp.int32, cube.shape, 0)
        iz = lax.broadcasted_iota(jnp.int32, cube.shape, 1)
        cube = cube + jnp.where(ix == 0, xp[comp][None], 0.0)
        cube = cube + jnp.where(ix == length_x - 1, xn[comp][None], 0.0)
        cube = cube + jnp.where(iz == 0, zp[comp][:, None, :], 0.0)
        cube = cube + jnp.where(iz == length_z - 1, zn[comp][:, None, :], 0.0)
        return cube.reshape(plane, length_y)

    def next_kernel(
        t_in, xp, xn, zp, zn, left_ref, right_ref, cols, share, u, t, xl, xh, zl, zh, sums
    ):
        sums[...] = jnp.zeros((8, length_y), jnp.float32)
        for comp in range(3):
            field = add_faces(comp, t_in, xp, xn, zp, zn)
            applied = apply(comp, field, left_ref, right_ref, cols, share, sums)
            store(comp, field, applied, u, t, xl, xh, zl, zh)

    devices = wall_count * lax.axis_size("span")

    def last_kernel(
        t_in, xp, xn, zp, zn, left_ref, right_ref, cols, share, sums_0, sums_1, u, moments, sums
    ):
        sums[...] = jnp.zeros((8, length_y), jnp.float32)
        for comp in range(3):
            field = add_faces(comp, t_in, xp, xn, zp, zn)
            apply(comp, field, left_ref, right_ref, cols, share, sums)
            u[comp] = field.reshape(length_x, length_z, length_y)
        stacked = jnp.concatenate([sums_0[...], sums_1[...], sums[...]], axis=0)
        total = jnp.sum(stacked, axis=1, keepdims=True)
        row = lax.broadcasted_iota(jnp.int32, (24, 18), 0)
        col = lax.broadcasted_iota(jnp.int32, (24, 18), 1)
        chosen = (row % 8 < 6) & (row // 8 * 6 + row % 8 == col)
        line = jnp.sum(jnp.where(chosen, total, 0.0), axis=0, keepdims=True)
        moments[...] = jnp.broadcast_to(line, (devices, 18))

    def combine_kernel(moments, u0, u1, u2, out):
        line = jnp.sum(moments[...], axis=0, keepdims=True)
        mu = [line[:, 3 * k : 3 * k + 3] for k in range(6)]

        def gram(poly, offset):
            value = None
            for i, first in enumerate(poly):
                for j, second in enumerate(poly):
                    term = first * second * mu[i + j + offset]
                    value = term if value is None else value + term
            return value

        one = jnp.ones((1, 3), jnp.float32)
        zero = jnp.zeros((1, 3), jnp.float32)
        residual, direction, answer = [one], [one], [zero, zero, zero]
        norm_now = mu[0]
        for sweep in range(3):
            step = norm_now / gram(direction, 1)
            for i, value in enumerate(direction):
                answer[i] = answer[i] + step * value
            if sweep < 2:
                residual = residual + [zero]
                residual = [residual[0]] + [
                    residual[i + 1] - step * value for i, value in enumerate(direction)
                ]
                norm_next = gram(residual, 0)
                growth = norm_next / norm_now
                direction = [
                    value + growth * direction[i] if i < len(direction) else value
                    for i, value in enumerate(residual)
                ]
                norm_now = norm_next
        for comp in range(3):
            coef = [value[:, comp : comp + 1] for value in answer]
            out[comp] = (
                (coef[0] * u0[comp].reshape(plane, length_y))
                + (coef[1] * u1[comp].reshape(plane, length_y))
                + (coef[2] * u2[comp].reshape(plane, length_y))
            ).reshape(length_x, length_z, length_y)

    tables = (left, right, columns, share_y)
    u0, t0, *faces, sums_0 = call(
        first_kernel, outs, velocity_old, traction, *around, spread_pick, *tables
    )
    u1, t1, *faces, sums_1 = call(next_kernel, outs, t0, *exchange(*faces), *tables)
    u2, moments, _ = call(
        last_kernel, [shape, (devices, 18), (8, length_y)],
        t1, *exchange(*faces), *tables, sums_0, sums_1,
    )
    moments = lax.all_to_all(moments, ("wall", "span"), 0, 0, tiled=True)
    (answer,) = call(combine_kernel, [shape], moments, u0, u1, u2)
    return (answer, neumann)


def solution(mesh):
    placed = (
        P(None, "wall", "span", None),
        P(),
        P(("wall", "span"), None),
        P(("wall", "span"), None),
        P(None, ("wall", "span")),
        P(("wall", "span")),
    )
    return jax.shard_map(
        body,
        mesh=mesh,
        in_specs=placed,
        out_specs=(P(None, "wall", "span", None), P(None, ("wall", "span"))),
        check_vma=False,
    )
```

```python
import jax
import jax.numpy as jnp
import numpy as np
from jax import lax
from jax.experimental import pallas as pl
from jax.experimental.pallas import tpu as pltpu
from jax.sharding import PartitionSpec as P

NEAR = 2


GLL_NODES = (
    -1.0,
    -0.8717401485096066,
    -0.5917001814331423,
    -0.2092992179024789,
    0.2092992179024789,
    0.5917001814331423,
    0.8717401485096066,
    1.0,
)
GLL_WEIGHTS = (
    0.03571428571428571,
    0.2107042271435061,
    0.3411226924835044,
    0.4124587946587038,
    0.4124587946587038,
    0.3411226924835044,
    0.2107042271435061,
    0.03571428571428571,
)
viscosity = 0.02
inverse_step = 20.0
karman = 0.41
sample_height = 0.1
speed_floor = 0.01
element_dx = 0.05
element_dz = 0.13
precise = lax.Precision.HIGHEST


def shifted(value, axis, steps):
    count = lax.axis_size(axis)
    pairs = [(source, (source + steps) % count) for source in range(count)]
    return lax.ppermute(value, axis, pairs)


def stiffness_table():
    points = np.array(GLL_NODES)
    weights = np.array(GLL_WEIGHTS)
    previous = np.ones(8)
    current = points.copy()
    for degree in range(1, 7):
        previous, current = (
            current,
            ((2 * degree + 1) * points * current - degree * previous) / (degree + 1),
        )
    derivative = np.zeros((8, 8))
    for target in range(8):
        for source in range(8):
            if target != source:
                derivative[target, source] = (
                    current[target] / current[source] / (points[target] - points[source])
                )
    derivative[0, 0] = -14.0
    derivative[7, 7] = 14.0
    return derivative.T @ (weights[:, None] * derivative)


def face_weights(length, open_ends):
    values = np.ones(length)
    position = np.arange(length) % 8
    values[(position == 0) | (position == 7)] = 0.5
    if open_ends:
        values[0] = 1.0
        values[-1] = 1.0
    return values


def join_matrix(length):
    table = np.eye(length)
    for node in range(7, length - 1, 8):
        table[node, node + 1] = 1.0
        table[node + 1, node] = 1.0
    return table


def exchange(x_low, x_high, z_low, z_high):
    from_prev = shifted(x_high, "wall", 1)
    from_next = shifted(x_low, "wall", -1)

    def with_corners(face, spot):
        first = face[:, :1] + from_prev[:, spot]
        last = face[:, -1:] + from_next[:, spot]
        return jnp.concatenate([first, face[:, 1:-1], last], axis=1)

    z_low = with_corners(z_low, slice(0, 1))
    z_high = with_corners(z_high, slice(-1, None))
    return from_prev, from_next, shifted(z_high, "span", 1), shifted(z_low, "span", -1)


def call(kernel, outs, *operands):
    space = pl.BlockSpec(memory_space=pltpu.VMEM)
    return pl.pallas_call(
        kernel,
        out_shape=[jax.ShapeDtypeStruct(shape, jnp.float32) for shape in outs],
        in_specs=[space] * len(operands),
        out_specs=[space] * len(outs),
    )(*operands)


def dot(first, second):
    return jnp.dot(first, second, precision=precise, preferred_element_type=jnp.float32)


def body(velocity_old, heights, owner_device, owner_element, ref_coords, roughness):
    weights = np.array(GLL_WEIGHTS)
    points = np.array(GLL_NODES)
    stiffness = stiffness_table()
    _, length_x, length_z, length_y = velocity_old.shape
    count_x, count_z, count_y = (length_x // 8, length_z // 8, length_y // 8)
    plane = length_x * length_z
    point_total = owner_device.shape[0]
    near = NEAR * 8

    mass_x = np.tile(0.5 * element_dx * weights, count_x)
    mass_z = np.tile(0.5 * element_dz * weights, count_z)
    stiff_x = np.kron(np.eye(count_x), stiffness * (2.0 / element_dx))
    stiff_z = np.kron(np.eye(count_z), stiffness * (2.0 / element_dz))
    join_x, join_z, join_y = (join_matrix(n) for n in (length_x, length_z, length_y))
    join_xz = np.kron(join_x, join_z)
    mass_xz = np.kron(mass_x, mass_z)
    plane_op = viscosity * (
        np.kron(stiff_x, np.diag(mass_z)) + np.kron(np.diag(mass_x), stiff_z)
    )
    left = jnp.asarray(
        np.concatenate([join_xz @ np.diag(mass_xz), join_xz @ plane_op], axis=1), jnp.float32
    )
    tiled = np.tile(weights, count_y)
    stiff_part = np.concatenate(
        [
            2.0 * viscosity * np.kron(np.eye(count_y), stiffness) @ join_y,
            np.zeros((length_y, length_y)),
        ],
        axis=1,
    ).reshape(count_y, 8, 2 * length_y)
    mass_part = np.concatenate(
        [inverse_step * 0.5 * tiled[:, None] * join_y, 0.5 * tiled[:, None] * join_y], axis=1
    ).reshape(count_y, 8, 2 * length_y)
    tall = heights[:, None, None]
    right = (
        jnp.asarray(stiff_part, jnp.float32) / tall + jnp.asarray(mass_part, jnp.float32) * tall
    ).reshape(length_y, 2 * length_y)

    def edge_sum(values):
        position = np.arange(values.shape[0]) % 8
        return np.where((position == 0) | (position == 7), 2.0 * values, values)

    columns = np.zeros((plane, 8))
    columns[:, 0] = np.kron(face_weights(length_x, False), face_weights(length_z, False))
    columns[:, 1] = np.kron(face_weights(length_x, True), face_weights(length_z, True))
    columns[:, 2] = inverse_step * np.kron(edge_sum(mass_x), edge_sum(mass_z))
    columns = jnp.asarray(columns, jnp.float32)
    share_y = jnp.asarray(face_weights(length_y, True)[None, :], jnp.float32)

    def packed_near():
        pieces = []
        for ex in range(count_x):
            for comp in (0, 2):
                block = velocity_old[comp, ex * 8 : ex * 8 + 8]
                pieces.append(block[:, :, :near])
                pieces.append(block[:, :, length_y - near :])
        return jnp.concatenate(pieces, axis=2).reshape(8 * length_z, count_x * 4 * near)

    own_near = packed_near()
    prev_near = shifted(own_near, "wall", 1)
    next_near = shifted(own_near, "wall", -1)
    wall_count = lax.axis_size("wall")
    own_wall = lax.axis_index("wall")
    distance = ((owner_device[:, 0] - own_wall + wall_count) % wall_count)[None, :]
    relation = jnp.where(distance == 1, 1.0, jnp.where(distance == 0, 0.0, -1.0))
    layer = (owner_element[:, 0] % count_y)[None, :]
    layer = jnp.where(layer < NEAR, layer, layer - (count_y - NEAR)).astype(jnp.float32)
    per_point = jnp.concatenate([ref_coords, relation, layer, roughness[None, :]], axis=0)
    lanes = count_x * 4 * near
    scale = 1.0 / np.prod(points[:, None] - points[None, :] + np.eye(8), axis=1)
    mass_row = jnp.asarray(mass_xz[None, :], jnp.float32)
    def sample_kernel(own, prev, nxt, info, mass, neu, trac):
        def basis(row):
            coord = info[row : row + 1, :]
            gaps = [coord - np.float32(p) for p in points]
            rows = []
            for a in range(8):
                value = None
                for b in range(8):
                    if b != a:
                        value = gaps[b] if value is None else value * gaps[b]
                rows.append(value * np.float32(scale[a]))
            return jnp.concatenate(rows, axis=0)

        along_x, along_z, along_y = basis(0), basis(1), basis(2)
        relation_row, layer_row = info[3:4, :], info[4:5, :]
        near_y = jnp.concatenate(
            [jnp.where(layer_row == np.float32(e), along_y, 0.0) for e in range(NEAR)], axis=0
        )
        full_y = jnp.concatenate([near_y] * (lanes // near), axis=0)
        row = lax.broadcasted_iota(jnp.int32, (lanes, point_total), 0)
        col = lax.broadcasted_iota(jnp.int32, (lanes, point_total), 1)
        fits = (row // (4 * near) == col % plane // (8 * length_z)) & (
            row // near % 2 == col // plane
        )
        comp = row // (2 * near) % 2
        zrow = lax.broadcasted_iota(jnp.int32, (8 * length_z, point_total), 0)
        zcol = lax.broadcasted_iota(jnp.int32, (8 * length_z, point_total), 1)
        tall_z = jnp.concatenate([along_z] * (count_z * 8), axis=0)
        tall_x = jnp.concatenate(
            [jnp.broadcast_to(along_x[a : a + 1, :], (length_z, point_total)) for a in range(8)],
            axis=0,
        )
        mix = jnp.where(zrow % length_z // 8 == zcol % length_z // 8, tall_z * tall_x, 0.0)
        sampled = []
        for k in range(2):
            table = jnp.where(fits & (comp == k), full_y, 0.0)
            picked = jnp.where(
                relation_row == 0.0,
                dot(own[...], table),
                jnp.where(relation_row > 0.0, dot(nxt[...], table), dot(prev[...], table)),
            )
            sampled.append(jnp.sum(picked * mix, axis=0, keepdims=True))
        stream, spanwise = sampled
        speed = jnp.sqrt(stream * stream + spanwise * spanwise + speed_floor)
        ratio = karman / jnp.log(sample_height / info[5:6, :])
        factor = -(ratio * ratio * speed / viscosity)
        neu[0:1, :] = factor * stream
        neu[1:2, :] = factor * spanwise
        half = []
        for value in (stream, spanwise):
            for side in range(2):
                part = (viscosity * (factor * value))[:, side * plane : (side + 1) * plane]
                half.append(part * mass[...])
        trac[...] = jnp.concatenate(half, axis=0)

    neumann, traction = call(
        sample_kernel,
        [(2, point_total), (4, plane)],
        own_near, prev_near, next_near, per_point, mass_row,
    )

    def plane_tables(length, mass, stiff):
        join = join_matrix(3 * length)
        wide_mass = join @ np.diag(np.tile(mass, 3)) @ join
        wide_stiff = join @ np.kron(np.eye(3), stiff) @ join
        return np.stack([join, wide_mass, wide_stiff])[:, length : 2 * length]

    ops_x = jnp.asarray(plane_tables(length_x, mass_x, stiff_x), jnp.float32)
    ops_z = jnp.asarray(plane_tables(length_z, mass_z, stiff_z), jnp.float32)
    wide = jnp.concatenate(
        [shifted(traction, "wall", 1), traction, shifted(traction, "wall", -1)], axis=1
    ).reshape(4, 3 * length_x, length_z)
    along = jnp.einsum("oxs,csz->ocxz", ops_x, wide, precision=precise)
    wide = jnp.concatenate(
        [shifted(along, "span", 1), along, shifted(along, "span", -1)], axis=3
    )
    both = jnp.einsum("ocxs,pzs->opcxz", wide, ops_z, precision=precise)
    walls = jnp.concatenate(
        [both[0, 0], both[1, 1], viscosity * (both[2, 1] + both[1, 2])], axis=0
    ).reshape(12, plane)

    shape = (3, length_x, length_z, length_y)
    x_face, z_face = (3, length_z, length_y), (3, length_x, length_y)
    halo = [shape, x_face, x_face, z_face, z_face]

    def apply(fields, left_ref, right_ref):
        both = dot(jnp.concatenate(fields, axis=0), right_ref[...])
        parts = [both[c * plane : (c + 1) * plane] for c in range(3)]
        stacked = jnp.concatenate(
            [
                jnp.concatenate([part[:, :length_y] for part in parts], axis=1),
                jnp.concatenate([part[:, length_y:] for part in parts], axis=1),
            ],
            axis=0,
        )
        applied = dot(left_ref[...], stacked)
        return [applied[:, c * length_y : (c + 1) * length_y] for c in range(3)]

    def total(first, second, weight, share):
        return share[...] * jnp.sum(first * second * weight, axis=0, keepdims=True)

    def store(comp, applied, t, xl, xh, zl, zh):
        cube = applied.reshape(length_x, length_z, length_y)
        t[comp] = cube
        xl[comp] = cube[0]
        xh[comp] = cube[length_x - 1]
        zl[comp] = cube[:, 0, :]
        zh[comp] = cube[:, length_z - 1, :]

    def smooth_part(comp, v, cols, right_ref):
        tall_y = jnp.sum(right_ref[:, length_y:], axis=0, keepdims=True)
        return v[comp].reshape(plane, length_y) * (cols[:, 2:3] * tall_y)

    def first_kernel(v, left_ref, right_ref, cols, t, xl, xh, zl, zh):
        fields = [smooth_part(comp, v, cols, right_ref) for comp in range(3)]
        for comp, applied in enumerate(apply(fields, left_ref, right_ref)):
            store(comp, applied, t, xl, xh, zl, zh)

    def add_faces(comp, t_in, xp, xn, zp, zn):
        cube = t_in[comp]
        ix = lax.broadcasted_iota(jnp.int32, cube.shape, 0)
        iz = lax.broadcasted_iota(jnp.int32, cube.shape, 1)
        cube = cube + jnp.where(ix == 0, xp[comp][None], 0.0)
        cube = cube + jnp.where(ix == length_x - 1, xn[comp][None], 0.0)
        cube = cube + jnp.where(iz == 0, zp[comp][:, None, :], 0.0)
        cube = cube + jnp.where(iz == length_z - 1, zn[comp][:, None, :], 0.0)
        return cube.reshape(plane, length_y)

    def next_kernel(
        v, wall_in, t_in, xp, xn, zp, zn, left_ref, right_ref, cols, share,
        u0, u1, t, xl, xh, zl, zh, sums,
    ):
        wall = jnp.concatenate([wall_in[...], jnp.zeros((4, plane), jnp.float32)], axis=0)
        wall = jnp.transpose(wall)
        lane = lax.broadcasted_iota(jnp.int32, (plane, length_y), 1)
        sums[...] = jnp.zeros((16, length_y), jnp.float32)
        fields = []
        for comp in range(3):
            base = smooth_part(comp, v, cols, right_ref)
            field = add_faces(comp, t_in, xp, xn, zp, zn)
            if comp != 1:
                for side, node in ((0, 0), (1, length_y - 1)):
                    at = comp + side
                    base = base + jnp.where(lane == node, wall[:, at : at + 1], 0.0)
                    line = right_ref[node : node + 1, :]
                    field = field + wall[:, at + 4 : at + 5] * line[:, :length_y]
                    field = field + wall[:, at + 8 : at + 9] * line[:, length_y:]
            u0[comp] = base.reshape(length_x, length_z, length_y)
            u1[comp] = field.reshape(length_x, length_z, length_y)
            weight = cols[:, 0:1]
            sums[comp : comp + 1, :] = total(base, base, weight, share)
            sums[comp + 3 : comp + 4, :] = total(base, field, weight, share)
            sums[comp + 6 : comp + 7, :] = total(field, field, weight, share)
            fields.append(field)
        for comp, applied in enumerate(apply(fields, left_ref, right_ref)):
            sums[comp + 9 : comp + 10, :] = total(fields[comp], applied, cols[:, 1:2], share)
            store(comp, applied, t, xl, xh, zl, zh)

    devices = wall_count * lax.axis_size("span")

    def last_kernel(
        t_in, xp, xn, zp, zn, left_ref, right_ref, cols, share, sums_1, u, moments
    ):
        fields = [add_faces(comp, t_in, xp, xn, zp, zn) for comp in range(3)]
        rows = [sums_1[...]]
        for comp, field in enumerate(fields):
            u[comp] = field.reshape(length_x, length_z, length_y)
            rows.append(total(field, field, cols[:, 0:1], share))
        for field, applied in zip(fields, apply(fields, left_ref, right_ref)):
            rows.append(total(field, applied, cols[:, 1:2], share))
        rows.append(jnp.zeros((2, length_y), jnp.float32))
        stacked = jnp.concatenate(rows, axis=0)
        summed = jnp.sum(stacked, axis=1, keepdims=True)
        row = lax.broadcasted_iota(jnp.int32, (24, 18), 0)
        col = lax.broadcasted_iota(jnp.int32, (24, 18), 1)
        chosen = ((row < 12) & (row == col)) | ((row >= 16) & (row - 4 == col))
        line = jnp.sum(jnp.where(chosen, summed, 0.0), axis=0, keepdims=True)
        moments[...] = jnp.broadcast_to(line, (devices, 18))

    def combine_kernel(moments, u0, u1, u2, out):
        line = jnp.sum(moments[...], axis=0, keepdims=True)
        mu = [line[:, 3 * k : 3 * k + 3] for k in range(6)]

        def gram(poly, offset):
            value = None
            for i, first in enumerate(poly):
                for j, second in enumerate(poly):
                    term = first * second * mu[i + j + offset]
                    value = term if value is None else value + term
            return value

        one = jnp.ones((1, 3), jnp.float32)
        zero = jnp.zeros((1, 3), jnp.float32)
        residual, direction, answer = [one], [one], [zero, zero, zero]
        norm_now = mu[0]
        for sweep in range(3):
            step = norm_now / gram(direction, 1)
            for i, value in enumerate(direction):
                answer[i] = answer[i] + step * value
            if sweep < 2:
                residual = residual + [zero]
                residual = [residual[0]] + [
                    residual[i + 1] - step * value for i, value in enumerate(direction)
                ]
                norm_next = gram(residual, 0)
                growth = norm_next / norm_now
                direction = [
                    value + growth * direction[i] if i < len(direction) else value
                    for i, value in enumerate(residual)
                ]
                norm_now = norm_next
        for comp in range(3):
            coef = [value[:, comp : comp + 1] for value in answer]
            out[comp] = (
                (coef[0] * u0[comp].reshape(plane, length_y))
                + (coef[1] * u1[comp].reshape(plane, length_y))
                + (coef[2] * u2[comp].reshape(plane, length_y))
            ).reshape(length_x, length_z, length_y)

    tables = (left, right, columns, share_y)
    t0, *faces = call(first_kernel, halo, velocity_old, *tables[:3])
    u0, u1, t1, *faces, sums_1 = call(
        next_kernel, [shape, shape, *halo, (16, length_y)],
        velocity_old, walls, t0, *exchange(*faces), *tables,
    )
    u2, moments = call(
        last_kernel, [shape, (devices, 18)], t1, *exchange(*faces), *tables, sums_1
    )
    moments = lax.all_to_all(moments, ("wall", "span"), 0, 0, tiled=True)
    (answer,) = call(combine_kernel, [shape], moments, u0, u1, u2)
    return (answer, neumann)


def solution(mesh):
    placed = (
        P(None, "wall", "span", None),
        P(),
        P(("wall", "span"), None),
        P(("wall", "span"), None),
        P(None, ("wall", "span")),
        P(("wall", "span")),
    )
    return jax.shard_map(
        body,
        mesh=mesh,
        in_specs=placed,
        out_specs=(P(None, "wall", "span", None), P(None, ("wall", "span"))),
        check_vma=False,
    )
```

```python
import jax
import jax.numpy as jnp
import numpy as np
from jax import lax
from jax.experimental import pallas as pl
from jax.experimental.pallas import tpu as pltpu
from jax.sharding import PartitionSpec as P

NEAR = 2


GLL_NODES = (
    -1.0,
    -0.8717401485096066,
    -0.5917001814331423,
    -0.2092992179024789,
    0.2092992179024789,
    0.5917001814331423,
    0.8717401485096066,
    1.0,
)
GLL_WEIGHTS = (
    0.03571428571428571,
    0.2107042271435061,
    0.3411226924835044,
    0.4124587946587038,
    0.4124587946587038,
    0.3411226924835044,
    0.2107042271435061,
    0.03571428571428571,
)
viscosity = 0.02
inverse_step = 20.0
karman = 0.41
sample_height = 0.1
speed_floor = 0.01
element_dx = 0.05
element_dz = 0.13
precise = lax.Precision.HIGHEST


def shifted(value, axis, steps):
    count = lax.axis_size(axis)
    pairs = [(source, (source + steps) % count) for source in range(count)]
    return lax.ppermute(value, axis, pairs)


def stiffness_table():
    points = np.array(GLL_NODES)
    weights = np.array(GLL_WEIGHTS)
    previous = np.ones(8)
    current = points.copy()
    for degree in range(1, 7):
        previous, current = (
            current,
            ((2 * degree + 1) * points * current - degree * previous) / (degree + 1),
        )
    derivative = np.zeros((8, 8))
    for target in range(8):
        for source in range(8):
            if target != source:
                derivative[target, source] = (
                    current[target] / current[source] / (points[target] - points[source])
                )
    derivative[0, 0] = -14.0
    derivative[7, 7] = 14.0
    return derivative.T @ (weights[:, None] * derivative)


def face_weights(length, open_ends):
    values = np.ones(length)
    position = np.arange(length) % 8
    values[(position == 0) | (position == 7)] = 0.5
    if open_ends:
        values[0] = 1.0
        values[-1] = 1.0
    return values


def join_matrix(length):
    table = np.eye(length)
    for node in range(7, length - 1, 8):
        table[node, node + 1] = 1.0
        table[node + 1, node] = 1.0
    return table


def face_corners(face, from_prev, from_next, spot):
    first = face[:, :1] + from_prev[:, spot]
    last = face[:, -1:] + from_next[:, spot]
    return jnp.concatenate([first, face[:, 1:-1], last], axis=1)


def exchange(x_low, x_high, z_low, z_high):
    from_prev = shifted(x_high, "wall", 1)
    from_next = shifted(x_low, "wall", -1)
    z_low = face_corners(z_low, from_prev, from_next, slice(0, 1))
    z_high = face_corners(z_high, from_prev, from_next, slice(-1, None))
    return from_prev, from_next, shifted(z_high, "span", 1), shifted(z_low, "span", -1)


def call(kernel, outs, *operands):
    space = pl.BlockSpec(memory_space=pltpu.VMEM)
    return pl.pallas_call(
        kernel,
        out_shape=[jax.ShapeDtypeStruct(shape, jnp.float32) for shape in outs],
        in_specs=[space] * len(operands),
        out_specs=[space] * len(outs),
    )(*operands)


def dot(first, second):
    return jnp.dot(first, second, precision=precise, preferred_element_type=jnp.float32)


def body(velocity_old, heights, owner_device, owner_element, ref_coords, roughness):
    weights = np.array(GLL_WEIGHTS)
    points = np.array(GLL_NODES)
    stiffness = stiffness_table()
    _, length_x, length_z, length_y = velocity_old.shape
    count_x, count_z, count_y = (length_x // 8, length_z // 8, length_y // 8)
    plane = length_x * length_z
    point_total = owner_device.shape[0]
    near = NEAR * 8

    mass_x = np.tile(0.5 * element_dx * weights, count_x)
    mass_z = np.tile(0.5 * element_dz * weights, count_z)
    stiff_x = np.kron(np.eye(count_x), stiffness * (2.0 / element_dx))
    stiff_z = np.kron(np.eye(count_z), stiffness * (2.0 / element_dz))
    join_z, join_y = (join_matrix(n) for n in (length_z, length_y))
    slab = 8 * length_z
    mass_xz = np.kron(mass_x, mass_z)
    mass_a, stiff_a = mass_x[:8], stiff_x[:8, :8]
    join_slab = np.kron(np.eye(8), join_z)
    slab_op = viscosity * (
        np.kron(stiff_a, np.diag(mass_z)) + np.kron(np.diag(mass_a), stiff_z)
    )
    left = jnp.asarray(
        np.concatenate(
            [join_slab @ np.diag(np.kron(mass_a, mass_z)), join_slab @ slab_op], axis=1
        ),
        jnp.float32,
    )
    tiled = np.tile(weights, count_y)
    stiff_part = np.concatenate(
        [
            2.0 * viscosity * np.kron(np.eye(count_y), stiffness) @ join_y,
            np.zeros((length_y, length_y)),
        ],
        axis=1,
    ).reshape(count_y, 8, 2 * length_y)
    mass_part = np.concatenate(
        [inverse_step * 0.5 * tiled[:, None] * join_y, 0.5 * tiled[:, None] * join_y], axis=1
    ).reshape(count_y, 8, 2 * length_y)
    tall = heights[:, None, None]
    right = (
        jnp.asarray(stiff_part, jnp.float32) / tall + jnp.asarray(mass_part, jnp.float32) * tall
    ).reshape(length_y, 2 * length_y)

    def edge_sum(values):
        position = np.arange(values.shape[0]) % 8
        return np.where((position == 0) | (position == 7), 2.0 * values, values)

    columns = np.zeros((plane, 8))
    columns[:, 0] = np.kron(face_weights(length_x, False), face_weights(length_z, False))
    columns[:, 1] = np.kron(face_weights(length_x, True), face_weights(length_z, True))
    columns[:, 2] = inverse_step * np.kron(edge_sum(mass_x), edge_sum(mass_z))
    columns = jnp.asarray(columns, jnp.float32)
    share_y = jnp.asarray(face_weights(length_y, True)[None, :], jnp.float32)

    wall_count = lax.axis_size("wall")
    own_wall = lax.axis_index("wall")
    distance = ((owner_device[:, 0] - own_wall + wall_count) % wall_count)[None, :]
    relation = jnp.where(distance == 1, 1.0, jnp.where(distance == 0, 0.0, -1.0))
    layer = (owner_element[:, 0] % count_y)[None, :]
    layer = jnp.where(layer < NEAR, layer, layer - (count_y - NEAR)).astype(jnp.float32)
    per_point = jnp.concatenate([ref_coords, relation, layer, roughness[None, :]], axis=0)
    lanes = count_x * 4 * near
    scale = 1.0 / np.prod(points[:, None] - points[None, :] + np.eye(8), axis=1)
    mass_row = jnp.asarray(mass_xz[None, :], jnp.float32)
    def sample_kernel(own, prev, nxt, info, mass, neu, trac):
        def basis(row):
            coord = info[row : row + 1, :]
            gaps = [coord - np.float32(p) for p in points]
            rows = []
            for a in range(8):
                value = None
                for b in range(8):
                    if b != a:
                        value = gaps[b] if value is None else value * gaps[b]
                rows.append(value * np.float32(scale[a]))
            return jnp.concatenate(rows, axis=0)

        along_x, along_z, along_y = basis(0), basis(1), basis(2)
        relation_row, layer_row = info[3:4, :], info[4:5, :]
        near_y = jnp.concatenate(
            [jnp.where(layer_row == np.float32(e), along_y, 0.0) for e in range(NEAR)], axis=0
        )
        full_y = jnp.concatenate([near_y] * (lanes // near), axis=0)
        row = lax.broadcasted_iota(jnp.int32, (lanes, point_total), 0)
        col = lax.broadcasted_iota(jnp.int32, (lanes, point_total), 1)
        fits = (row // (4 * near) == col % plane // (8 * length_z)) & (
            row // near % 2 == col // plane
        )
        comp = row // (2 * near) % 2
        zrow = lax.broadcasted_iota(jnp.int32, (8 * length_z, point_total), 0)
        zcol = lax.broadcasted_iota(jnp.int32, (8 * length_z, point_total), 1)
        tall_z = jnp.concatenate([along_z] * (count_z * 8), axis=0)
        tall_x = jnp.concatenate(
            [jnp.broadcast_to(along_x[a : a + 1, :], (length_z, point_total)) for a in range(8)],
            axis=0,
        )
        mix = jnp.where(zrow % length_z // 8 == zcol % length_z // 8, tall_z * tall_x, 0.0)
        sampled = []
        for k in range(2):
            table = jnp.where(fits & (comp == k), full_y, 0.0)
            picked = jnp.where(
                relation_row == 0.0,
                dot(own[:slab, :], table),
                jnp.where(relation_row > 0.0, dot(nxt[:slab, :], table), dot(prev[:slab, :], table)),
            )
            sampled.append(jnp.sum(picked * mix, axis=0, keepdims=True))
        stream, spanwise = sampled
        speed = jnp.sqrt(stream * stream + spanwise * spanwise + speed_floor)
        ratio = karman / jnp.log(sample_height / info[5:6, :])
        factor = -(ratio * ratio * speed / viscosity)
        neu[0:1, :] = factor * stream
        neu[1:2, :] = factor * spanwise
        half = []
        for value in (stream, spanwise):
            for side in range(2):
                part = (viscosity * (factor * value))[:, side * plane : (side + 1) * plane]
                half.append(part * mass[...])
        trac[...] = jnp.concatenate(half, axis=0)

    shape = (3, length_x, length_z, length_y)
    x_face, z_face = (3, length_z, length_y), (3, length_x, length_y)
    halo = [shape, x_face, x_face, z_face, z_face]
    face_rows = 3 * length_z
    message = (slab + face_rows, length_y)

    def apply(fields, left_ref, right_ref):
        both = dot(jnp.concatenate(fields, axis=0), right_ref[...])
        parts = [both[k * slab : (k + 1) * slab] for k in range(3 * count_x)]
        stacked = jnp.concatenate(
            [
                jnp.concatenate([part[:, :length_y] for part in parts], axis=1),
                jnp.concatenate([part[:, length_y:] for part in parts], axis=1),
            ],
            axis=0,
        )
        applied = dot(left_ref[...], stacked)
        joined = []
        for c in range(3):
            pieces = []
            for ex in range(count_x):
                k = c * count_x + ex
                pieces.append(applied[:, k * length_y : (k + 1) * length_y])
            rows = []
            for ex, piece in enumerate(pieces):
                first, last = piece[:length_z], piece[slab - length_z :]
                if ex > 0:
                    first = first + pieces[ex - 1][slab - length_z :]
                if ex + 1 < count_x:
                    last = last + pieces[ex + 1][:length_z]
                rows += [first, piece[length_z : slab - length_z], last]
            joined.append(jnp.concatenate(rows, axis=0))
        return joined

    def total(first, second, weight, share):
        return share[...] * jnp.sum(first * second * weight, axis=0, keepdims=True)

    def store(comp, applied, t, xl, xh, zl, zh):
        cube = applied.reshape(length_x, length_z, length_y)
        t[comp] = cube
        xl[comp] = cube[0]
        xh[comp] = cube[length_x - 1]
        zl[comp] = cube[:, 0, :]
        zh[comp] = cube[:, length_z - 1, :]

    def smooth_part(comp, v, cols, right_ref):
        tall_y = jnp.sum(right_ref[:, length_y:], axis=0, keepdims=True)
        return v[comp].reshape(plane, length_y) * (cols[:, 2:3] * tall_y)

    def first_kernel(v, left_ref, right_ref, cols, t, low, high, zl, zh):
        near_parts = []
        for ex in range(count_x):
            for comp in (0, 2):
                block = v[comp, ex * 8 : ex * 8 + 8].reshape(slab, length_y)
                near_parts += [block[:, :near], block[:, length_y - near :]]
        near_all = jnp.concatenate(near_parts, axis=1)
        low[:slab, :] = near_all
        high[:slab, :] = near_all
        fields = [smooth_part(comp, v, cols, right_ref) for comp in range(3)]
        for comp, applied in enumerate(apply(fields, left_ref, right_ref)):
            cube = applied.reshape(length_x, length_z, length_y)
            t[comp] = cube
            at = slab + comp * length_z
            low[at : at + length_z, :] = cube[0]
            high[at : at + length_z, :] = cube[length_x - 1]
            zl[comp] = cube[:, 0, :]
            zh[comp] = cube[:, length_z - 1, :]

    def add_faces(comp, t_in, xp, xn, zp, zn):
        cube = t_in[comp]
        ix = lax.broadcasted_iota(jnp.int32, cube.shape, 0)
        iz = lax.broadcasted_iota(jnp.int32, cube.shape, 1)
        cube = cube + jnp.where(ix == 0, xp[comp][None], 0.0)
        cube = cube + jnp.where(ix == length_x - 1, xn[comp][None], 0.0)
        cube = cube + jnp.where(iz == 0, zp[comp][:, None, :], 0.0)
        cube = cube + jnp.where(iz == length_z - 1, zn[comp][:, None, :], 0.0)
        return cube.reshape(plane, length_y)

    def next_kernel(
        v, wall_in, t_in, xp, xn, zp, zn, left_ref, right_ref, cols, share,
        u0, u1, t, xl, xh, zl, zh, sums,
    ):
        wall = jnp.concatenate([wall_in[...], jnp.zeros((4, plane), jnp.float32)], axis=0)
        wall = jnp.transpose(wall)
        lane = lax.broadcasted_iota(jnp.int32, (plane, length_y), 1)
        sums[...] = jnp.zeros((16, length_y), jnp.float32)
        fields = []
        for comp in range(3):
            base = smooth_part(comp, v, cols, right_ref)
            field = add_faces(comp, t_in, xp, xn, zp, zn)
            if comp != 1:
                for side, node in ((0, 0), (1, length_y - 1)):
                    at = comp + side
                    base = base + jnp.where(lane == node, wall[:, at : at + 1], 0.0)
                    line = right_ref[node : node + 1, :]
                    field = field + wall[:, at + 4 : at + 5] * line[:, :length_y]
                    field = field + wall[:, at + 8 : at + 9] * line[:, length_y:]
            u0[comp] = base.reshape(length_x, length_z, length_y)
            u1[comp] = field.reshape(length_x, length_z, length_y)
            weight = cols[:, 0:1]
            sums[comp : comp + 1, :] = total(base, base, weight, share)
            sums[comp + 3 : comp + 4, :] = total(base, field, weight, share)
            sums[comp + 6 : comp + 7, :] = total(field, field, weight, share)
            fields.append(field)
        for comp, applied in enumerate(apply(fields, left_ref, right_ref)):
            sums[comp + 9 : comp + 10, :] = total(fields[comp], applied, cols[:, 1:2], share)
            store(comp, applied, t, xl, xh, zl, zh)

    devices = wall_count * lax.axis_size("span")

    def last_kernel(
        t_in, xp, xn, zp, zn, left_ref, right_ref, cols, share, sums_1, u, moments
    ):
        fields = [add_faces(comp, t_in, xp, xn, zp, zn) for comp in range(3)]
        rows = [sums_1[...]]
        for comp, field in enumerate(fields):
            u[comp] = field.reshape(length_x, length_z, length_y)
            rows.append(total(field, field, cols[:, 0:1], share))
        for field, applied in zip(fields, apply(fields, left_ref, right_ref)):
            rows.append(total(field, applied, cols[:, 1:2], share))
        rows.append(jnp.zeros((2, length_y), jnp.float32))
        stacked = jnp.concatenate(rows, axis=0)
        summed = jnp.sum(stacked, axis=1, keepdims=True)
        row = lax.broadcasted_iota(jnp.int32, (24, 18), 0)
        col = lax.broadcasted_iota(jnp.int32, (24, 18), 1)
        chosen = ((row < 12) & (row == col)) | ((row >= 16) & (row - 4 == col))
        line = jnp.sum(jnp.where(chosen, summed, 0.0), axis=0, keepdims=True)
        moments[...] = jnp.broadcast_to(line, (devices, 18))

    def combine_kernel(moments, u0, u1, u2, out):
        line = jnp.sum(moments[...], axis=0, keepdims=True)
        mu = [line[:, 3 * k : 3 * k + 3] for k in range(6)]

        def gram(poly, offset):
            value = None
            for i, first in enumerate(poly):
                for j, second in enumerate(poly):
                    term = first * second * mu[i + j + offset]
                    value = term if value is None else value + term
            return value

        one = jnp.ones((1, 3), jnp.float32)
        zero = jnp.zeros((1, 3), jnp.float32)
        residual, direction, answer = [one], [one], [zero, zero, zero]
        norm_now = mu[0]
        for sweep in range(3):
            step = norm_now / gram(direction, 1)
            for i, value in enumerate(direction):
                answer[i] = answer[i] + step * value
            if sweep < 2:
                residual = residual + [zero]
                residual = [residual[0]] + [
                    residual[i + 1] - step * value for i, value in enumerate(direction)
                ]
                norm_next = gram(residual, 0)
                growth = norm_next / norm_now
                direction = [
                    value + growth * direction[i] if i < len(direction) else value
                    for i, value in enumerate(residual)
                ]
                norm_now = norm_next
        for comp in range(3):
            coef = [value[:, comp : comp + 1] for value in answer]
            out[comp] = (
                (coef[0] * u0[comp].reshape(plane, length_y))
                + (coef[1] * u1[comp].reshape(plane, length_y))
                + (coef[2] * u2[comp].reshape(plane, length_y))
            ).reshape(length_x, length_z, length_y)

    tables = (left, right, columns, share_y)
    t0, low, high, z_low, z_high = call(
        first_kernel, [shape, message, message, z_face, z_face], velocity_old, *tables[:3]
    )
    from_prev = shifted(high, "wall", 1)
    from_next = shifted(low, "wall", -1)
    neumann, traction = call(
        sample_kernel,
        [(2, point_total), (4, plane)],
        low, from_prev, from_next, per_point, mass_row,
    )

    def plane_tables(length, mass, stiff):
        join = join_matrix(3 * length)
        wide_mass = join @ np.diag(np.tile(mass, 3)) @ join
        wide_stiff = join @ np.kron(np.eye(3), stiff) @ join
        return np.stack([join, wide_mass, wide_stiff])[:, length : 2 * length]

    ops_x = jnp.asarray(plane_tables(length_x, mass_x, stiff_x), jnp.float32)
    ops_z = jnp.asarray(plane_tables(length_z, mass_z, stiff_z), jnp.float32)
    wide = jnp.concatenate(
        [shifted(traction, "wall", 1), traction, shifted(traction, "wall", -1)], axis=1
    ).reshape(4, 3 * length_x, length_z)
    along = jnp.einsum("oxs,csz->ocxz", ops_x, wide, precision=precise)
    size = along.size // length_y
    along_rows = along.reshape(size, length_y)
    x_prev = from_prev[slab:].reshape(x_face)
    x_next = from_next[slab:].reshape(x_face)

    def z_message(face, spot):
        face = face_corners(face, x_prev, x_next, spot)
        return jnp.concatenate([along_rows, face.reshape(3 * length_x, length_y)], axis=0)

    z_prev = shifted(z_message(z_high, slice(-1, None)), "span", 1)
    z_next = shifted(z_message(z_low, slice(0, 1)), "span", -1)
    wide = jnp.concatenate(
        [z_prev[:size].reshape(along.shape), along, z_next[:size].reshape(along.shape)], axis=3
    )
    around = (x_prev, x_next, z_prev[size:].reshape(z_face), z_next[size:].reshape(z_face))
    both = jnp.einsum("ocxs,pzs->opcxz", wide, ops_z, precision=precise)
    walls = jnp.concatenate(
        [both[0, 0], both[1, 1], viscosity * (both[2, 1] + both[1, 2])], axis=0
    ).reshape(12, plane)

    u0, u1, t1, *faces, sums_1 = call(
        next_kernel, [shape, shape, *halo, (16, length_y)],
        velocity_old, walls, t0, *around, *tables,
    )
    u2, moments = call(
        last_kernel, [shape, (devices, 18)], t1, *exchange(*faces), *tables, sums_1
    )
    moments = lax.all_to_all(moments, ("wall", "span"), 0, 0, tiled=True)
    (answer,) = call(combine_kernel, [shape], moments, u0, u1, u2)
    return (answer, neumann)


def solution(mesh):
    placed = (
        P(None, "wall", "span", None),
        P(),
        P(("wall", "span"), None),
        P(("wall", "span"), None),
        P(None, ("wall", "span")),
        P(("wall", "span")),
    )
    return jax.shard_map(
        body,
        mesh=mesh,
        in_specs=placed,
        out_specs=(P(None, "wall", "span", None), P(None, ("wall", "span"))),
        check_vma=False,
    )
```

```python
import jax
import jax.numpy as jnp
import numpy as np
from jax import lax
from jax.experimental import pallas as pl
from jax.experimental.pallas import tpu as pltpu
from jax.sharding import PartitionSpec as P

NEAR = 2


GLL_NODES = (
    -1.0,
    -0.8717401485096066,
    -0.5917001814331423,
    -0.2092992179024789,
    0.2092992179024789,
    0.5917001814331423,
    0.8717401485096066,
    1.0,
)
GLL_WEIGHTS = (
    0.03571428571428571,
    0.2107042271435061,
    0.3411226924835044,
    0.4124587946587038,
    0.4124587946587038,
    0.3411226924835044,
    0.2107042271435061,
    0.03571428571428571,
)
viscosity = 0.02
inverse_step = 20.0
karman = 0.41
sample_height = 0.1
speed_floor = 0.01
element_dx = 0.05
element_dz = 0.13
precise = lax.Precision.HIGHEST


def shifted(value, axis, steps):
    count = lax.axis_size(axis)
    pairs = [(source, (source + steps) % count) for source in range(count)]
    return lax.ppermute(value, axis, pairs)


def stiffness_table():
    points = np.array(GLL_NODES)
    weights = np.array(GLL_WEIGHTS)
    previous = np.ones(8)
    current = points.copy()
    for degree in range(1, 7):
        previous, current = (
            current,
            ((2 * degree + 1) * points * current - degree * previous) / (degree + 1),
        )
    derivative = np.zeros((8, 8))
    for target in range(8):
        for source in range(8):
            if target != source:
                derivative[target, source] = (
                    current[target] / current[source] / (points[target] - points[source])
                )
    derivative[0, 0] = -14.0
    derivative[7, 7] = 14.0
    return derivative.T @ (weights[:, None] * derivative)


def face_weights(length, open_ends):
    values = np.ones(length)
    position = np.arange(length) % 8
    values[(position == 0) | (position == 7)] = 0.5
    if open_ends:
        values[0] = 1.0
        values[-1] = 1.0
    return values


def join_matrix(length):
    table = np.eye(length)
    for node in range(7, length - 1, 8):
        table[node, node + 1] = 1.0
        table[node + 1, node] = 1.0
    return table


def face_corners(face, from_prev, from_next, spot):
    first = face[:, :1] + from_prev[:, spot]
    last = face[:, -1:] + from_next[:, spot]
    return jnp.concatenate([first, face[:, 1:-1], last], axis=1)


def exchange(x_low, x_high, z_low, z_high):
    from_prev = shifted(x_high, "wall", 1)
    from_next = shifted(x_low, "wall", -1)
    z_low = face_corners(z_low, from_prev, from_next, slice(0, 1))
    z_high = face_corners(z_high, from_prev, from_next, slice(-1, None))
    return from_prev, from_next, shifted(z_high, "span", 1), shifted(z_low, "span", -1)


def call(kernel, outs, *operands):
    space = pl.BlockSpec(memory_space=pltpu.VMEM)
    return pl.pallas_call(
        kernel,
        out_shape=[jax.ShapeDtypeStruct(shape, jnp.float32) for shape in outs],
        in_specs=[space] * len(operands),
        out_specs=[space] * len(outs),
    )(*operands)


def dot(first, second):
    return jnp.dot(first, second, precision=precise, preferred_element_type=jnp.float32)


def body(velocity_old, heights, owner_device, owner_element, ref_coords, roughness):
    weights = np.array(GLL_WEIGHTS)
    points = np.array(GLL_NODES)
    stiffness = stiffness_table()
    _, length_x, length_z, length_y = velocity_old.shape
    count_x, count_z, count_y = (length_x // 8, length_z // 8, length_y // 8)
    plane = length_x * length_z
    point_total = owner_device.shape[0]
    near = NEAR * 8

    mass_x = np.tile(0.5 * element_dx * weights, count_x)
    mass_z = np.tile(0.5 * element_dz * weights, count_z)
    stiff_x = np.kron(np.eye(count_x), stiffness * (2.0 / element_dx))
    stiff_z = np.kron(np.eye(count_z), stiffness * (2.0 / element_dz))
    join_z, join_y = (join_matrix(n) for n in (length_z, length_y))
    slab = 8 * length_z
    mass_xz = np.kron(mass_x, mass_z)
    mass_a, stiff_a = mass_x[:8], stiff_x[:8, :8]
    join_slab = np.kron(np.eye(8), join_z)
    slab_op = viscosity * (
        np.kron(stiff_a, np.diag(mass_z)) + np.kron(np.diag(mass_a), stiff_z)
    )
    left = jnp.asarray(
        np.concatenate(
            [join_slab @ np.diag(np.kron(mass_a, mass_z)), join_slab @ slab_op], axis=1
        ),
        jnp.float32,
    )
    tiled = np.tile(weights, count_y)
    stiff_part = np.concatenate(
        [
            2.0 * viscosity * np.kron(np.eye(count_y), stiffness) @ join_y,
            np.zeros((length_y, length_y)),
        ],
        axis=1,
    ).reshape(count_y, 8, 2 * length_y)
    mass_part = np.concatenate(
        [inverse_step * 0.5 * tiled[:, None] * join_y, 0.5 * tiled[:, None] * join_y], axis=1
    ).reshape(count_y, 8, 2 * length_y)
    tall = heights[:, None, None]
    right = (
        jnp.asarray(stiff_part, jnp.float32) / tall + jnp.asarray(mass_part, jnp.float32) * tall
    ).reshape(length_y, 2 * length_y)

    def edge_sum(values):
        position = np.arange(values.shape[0]) % 8
        return np.where((position == 0) | (position == 7), 2.0 * values, values)

    columns = np.zeros((plane, 8))
    columns[:, 0] = np.kron(face_weights(length_x, False), face_weights(length_z, False))
    columns[:, 1] = np.kron(face_weights(length_x, True), face_weights(length_z, True))
    columns[:, 2] = inverse_step * np.kron(edge_sum(mass_x), edge_sum(mass_z))
    columns = jnp.asarray(columns, jnp.float32)
    share_y = jnp.asarray(face_weights(length_y, True)[None, :], jnp.float32)

    wall_count = lax.axis_size("wall")
    own_wall = lax.axis_index("wall")
    distance = ((owner_device[:, 0] - own_wall + wall_count) % wall_count)[None, :]
    relation = jnp.where(distance == 1, 1.0, jnp.where(distance == 0, 0.0, -1.0))
    layer = (owner_element[:, 0] % count_y)[None, :]
    layer = jnp.where(layer < NEAR, layer, layer - (count_y - NEAR)).astype(jnp.float32)
    per_point = jnp.concatenate([ref_coords, relation, layer, roughness[None, :]], axis=0)
    lanes = count_x * 4 * near
    scale = 1.0 / np.prod(points[:, None] - points[None, :] + np.eye(8), axis=1)
    mass_row = jnp.asarray(mass_xz[None, :], jnp.float32)
    def sample_kernel(own, prev, nxt, info, mass, neu, trac):
        def basis(row):
            coord = info[row : row + 1, :]
            gaps = [coord - np.float32(p) for p in points]
            rows = []
            for a in range(8):
                value = None
                for b in range(8):
                    if b != a:
                        value = gaps[b] if value is None else value * gaps[b]
                rows.append(value * np.float32(scale[a]))
            return jnp.concatenate(rows, axis=0)

        along_x, along_z, along_y = basis(0), basis(1), basis(2)
        relation_row, layer_row = info[3:4, :], info[4:5, :]
        near_y = jnp.concatenate(
            [jnp.where(layer_row == np.float32(e), along_y, 0.0) for e in range(NEAR)], axis=0
        )
        full_y = jnp.concatenate([near_y] * (lanes // near), axis=0)
        row = lax.broadcasted_iota(jnp.int32, (lanes, point_total), 0)
        col = lax.broadcasted_iota(jnp.int32, (lanes, point_total), 1)
        fits = (row // (4 * near) == col % plane // (8 * length_z)) & (
            row // near % 2 == col // plane
        )
        comp = row // (2 * near) % 2
        zrow = lax.broadcasted_iota(jnp.int32, (8 * length_z, point_total), 0)
        zcol = lax.broadcasted_iota(jnp.int32, (8 * length_z, point_total), 1)
        tall_z = jnp.concatenate([along_z] * (count_z * 8), axis=0)
        tall_x = jnp.concatenate(
            [jnp.broadcast_to(along_x[a : a + 1, :], (length_z, point_total)) for a in range(8)],
            axis=0,
        )
        mix = jnp.where(zrow % length_z // 8 == zcol % length_z // 8, tall_z * tall_x, 0.0)
        sampled = []
        for k in range(2):
            table = jnp.where(fits & (comp == k), full_y, 0.0)
            picked = jnp.where(
                relation_row == 0.0,
                dot(own[:slab, :], table),
                jnp.where(relation_row > 0.0, dot(nxt[:slab, :], table), dot(prev[:slab, :], table)),
            )
            sampled.append(jnp.sum(picked * mix, axis=0, keepdims=True))
        stream, spanwise = sampled
        speed = jnp.sqrt(stream * stream + spanwise * spanwise + speed_floor)
        ratio = karman / jnp.log(sample_height / info[5:6, :])
        factor = -(ratio * ratio * speed / viscosity)
        neu[0:1, :] = factor * stream
        neu[1:2, :] = factor * spanwise
        half = []
        for value in (stream, spanwise):
            for side in range(2):
                part = (viscosity * (factor * value))[:, side * plane : (side + 1) * plane]
                half.append(part * mass[...])
        trac[...] = jnp.concatenate(half, axis=0)

    shape = (3, length_x, length_z, length_y)
    x_face, z_face = (3, length_z, length_y), (3, length_x, length_y)
    halo = [shape, x_face, x_face, z_face, z_face]
    face_rows = 3 * length_z
    message = (slab + face_rows, length_y)

    def apply(fields, left_ref, right_ref):
        both = dot(jnp.concatenate(fields, axis=0), right_ref[...])
        parts = [both[k * slab : (k + 1) * slab] for k in range(3 * count_x)]
        stacked = jnp.concatenate(
            [
                jnp.concatenate([part[:, :length_y] for part in parts], axis=1),
                jnp.concatenate([part[:, length_y:] for part in parts], axis=1),
            ],
            axis=0,
        )
        applied = dot(left_ref[...], stacked)
        joined = []
        for c in range(3):
            pieces = []
            for ex in range(count_x):
                k = c * count_x + ex
                pieces.append(applied[:, k * length_y : (k + 1) * length_y])
            rows = []
            for ex, piece in enumerate(pieces):
                first, last = piece[:length_z], piece[slab - length_z :]
                if ex > 0:
                    first = first + pieces[ex - 1][slab - length_z :]
                if ex + 1 < count_x:
                    last = last + pieces[ex + 1][:length_z]
                rows += [first, piece[length_z : slab - length_z], last]
            joined.append(jnp.concatenate(rows, axis=0))
        return joined

    def total(first, second, weight, share):
        return share[...] * jnp.sum(first * second * weight, axis=0, keepdims=True)

    def store(comp, applied, t, xl, xh, zl, zh):
        cube = applied.reshape(length_x, length_z, length_y)
        t[comp] = cube
        xl[comp] = cube[0]
        xh[comp] = cube[length_x - 1]
        zl[comp] = cube[:, 0, :]
        zh[comp] = cube[:, length_z - 1, :]

    def smooth_part(comp, v, cols, right_ref):
        tall_y = jnp.sum(right_ref[:, length_y:], axis=0, keepdims=True)
        return v[comp].reshape(plane, length_y) * (cols[:, 2:3] * tall_y)

    def first_kernel(v, left_ref, right_ref, cols, t, low, high, zl, zh):
        near_parts = []
        for ex in range(count_x):
            for comp in (0, 2):
                block = v[comp, ex * 8 : ex * 8 + 8].reshape(slab, length_y)
                near_parts += [block[:, :near], block[:, length_y - near :]]
        near_all = jnp.concatenate(near_parts, axis=1)
        low[:slab, :] = near_all
        high[:slab, :] = near_all
        fields = [smooth_part(comp, v, cols, right_ref) for comp in range(3)]
        for comp, applied in enumerate(apply(fields, left_ref, right_ref)):
            cube = applied.reshape(length_x, length_z, length_y)
            t[comp] = cube
            at = slab + comp * length_z
            low[at : at + length_z, :] = cube[0]
            high[at : at + length_z, :] = cube[length_x - 1]
            zl[comp] = cube[:, 0, :]
            zh[comp] = cube[:, length_z - 1, :]

    def add_faces(comp, t_in, xp, xn, zp, zn):
        cube = t_in[comp]
        ix = lax.broadcasted_iota(jnp.int32, cube.shape, 0)
        iz = lax.broadcasted_iota(jnp.int32, cube.shape, 1)
        cube = cube + jnp.where(ix == 0, xp[comp][None], 0.0)
        cube = cube + jnp.where(ix == length_x - 1, xn[comp][None], 0.0)
        cube = cube + jnp.where(iz == 0, zp[comp][:, None, :], 0.0)
        cube = cube + jnp.where(iz == length_z - 1, zn[comp][:, None, :], 0.0)
        return cube.reshape(plane, length_y)

    def next_kernel(
        v, wall_in, t_in, xp, xn, zp, zn, left_ref, right_ref, cols, share,
        u0, u1, t, xl, xh, zl, zh, sums,
    ):
        wall = jnp.concatenate([wall_in[...], jnp.zeros((4, plane), jnp.float32)], axis=0)
        wall = jnp.transpose(wall)
        lane = lax.broadcasted_iota(jnp.int32, (plane, length_y), 1)
        sums[...] = jnp.zeros((16, length_y), jnp.float32)
        fields = []
        xp, xn = (
            [m[slab + c * length_z : slab + (c + 1) * length_z, :] for c in range(3)]
            for m in (xp, xn)
        )
        zp, zn = (
            [m[size + c * length_x : size + (c + 1) * length_x, :] for c in range(3)]
            for m in (zp, zn)
        )
        for comp in range(3):
            base = smooth_part(comp, v, cols, right_ref)
            field = add_faces(comp, t_in, xp, xn, zp, zn)
            if comp != 1:
                for side, node in ((0, 0), (1, length_y - 1)):
                    at = comp + side
                    base = base + jnp.where(lane == node, wall[:, at : at + 1], 0.0)
                    line = right_ref[node : node + 1, :]
                    field = field + wall[:, at + 4 : at + 5] * line[:, :length_y]
                    field = field + wall[:, at + 8 : at + 9] * line[:, length_y:]
            u0[comp] = base.reshape(length_x, length_z, length_y)
            u1[comp] = field.reshape(length_x, length_z, length_y)
            weight = cols[:, 0:1]
            sums[comp : comp + 1, :] = total(base, base, weight, share)
            sums[comp + 3 : comp + 4, :] = total(base, field, weight, share)
            sums[comp + 6 : comp + 7, :] = total(field, field, weight, share)
            fields.append(field)
        for comp, applied in enumerate(apply(fields, left_ref, right_ref)):
            sums[comp + 9 : comp + 10, :] = total(fields[comp], applied, cols[:, 1:2], share)
            store(comp, applied, t, xl, xh, zl, zh)

    devices = wall_count * lax.axis_size("span")

    def last_kernel(
        t_in, xp, xn, zp, zn, left_ref, right_ref, cols, share, sums_1, u, moments
    ):
        fields = [add_faces(comp, t_in, xp, xn, zp, zn) for comp in range(3)]
        rows = [sums_1[...]]
        for comp, field in enumerate(fields):
            u[comp] = field.reshape(length_x, length_z, length_y)
            rows.append(total(field, field, cols[:, 0:1], share))
        for field, applied in zip(fields, apply(fields, left_ref, right_ref)):
            rows.append(total(field, applied, cols[:, 1:2], share))
        rows.append(jnp.zeros((2, length_y), jnp.float32))
        stacked = jnp.concatenate(rows, axis=0)
        summed = jnp.sum(stacked, axis=1, keepdims=True)
        row = lax.broadcasted_iota(jnp.int32, (24, 18), 0)
        col = lax.broadcasted_iota(jnp.int32, (24, 18), 1)
        chosen = ((row < 12) & (row == col)) | ((row >= 16) & (row - 4 == col))
        line = jnp.sum(jnp.where(chosen, summed, 0.0), axis=0, keepdims=True)
        moments[...] = jnp.broadcast_to(line, (devices, 18))

    def combine_kernel(moments, u0, u1, u2, out):
        line = jnp.sum(moments[...], axis=0, keepdims=True)
        mu = [line[:, 3 * k : 3 * k + 3] for k in range(6)]

        def gram(poly, offset):
            value = None
            for i, first in enumerate(poly):
                for j, second in enumerate(poly):
                    term = first * second * mu[i + j + offset]
                    value = term if value is None else value + term
            return value

        one = jnp.ones((1, 3), jnp.float32)
        zero = jnp.zeros((1, 3), jnp.float32)
        residual, direction, answer = [one], [one], [zero, zero, zero]
        norm_now = mu[0]
        for sweep in range(3):
            step = norm_now / gram(direction, 1)
            for i, value in enumerate(direction):
                answer[i] = answer[i] + step * value
            if sweep < 2:
                residual = residual + [zero]
                residual = [residual[0]] + [
                    residual[i + 1] - step * value for i, value in enumerate(direction)
                ]
                norm_next = gram(residual, 0)
                growth = norm_next / norm_now
                direction = [
                    value + growth * direction[i] if i < len(direction) else value
                    for i, value in enumerate(residual)
                ]
                norm_now = norm_next
        for comp in range(3):
            coef = [value[:, comp : comp + 1] for value in answer]
            out[comp] = (
                (coef[0] * u0[comp].reshape(plane, length_y))
                + (coef[1] * u1[comp].reshape(plane, length_y))
                + (coef[2] * u2[comp].reshape(plane, length_y))
            ).reshape(length_x, length_z, length_y)

    tables = (left, right, columns, share_y)
    t0, low, high, z_low, z_high = call(
        first_kernel, [shape, message, message, z_face, z_face], velocity_old, *tables[:3]
    )
    from_prev = shifted(high, "wall", 1)
    from_next = shifted(low, "wall", -1)
    neumann, traction = call(
        sample_kernel,
        [(2, point_total), (4, plane)],
        low, from_prev, from_next, per_point, mass_row,
    )

    def plane_tables(length, mass, stiff):
        join = join_matrix(3 * length)
        wide_mass = join @ np.diag(np.tile(mass, 3)) @ join
        wide_stiff = join @ np.kron(np.eye(3), stiff) @ join
        return np.stack([join, wide_mass, wide_stiff])[:, length : 2 * length]

    ops_x = jnp.asarray(plane_tables(length_x, mass_x, stiff_x), jnp.float32)
    ops_z = jnp.asarray(plane_tables(length_z, mass_z, stiff_z), jnp.float32)
    wide = jnp.concatenate(
        [shifted(traction, "wall", 1), traction, shifted(traction, "wall", -1)], axis=1
    ).reshape(4, 3 * length_x, length_z)
    along = jnp.einsum("oxs,csz->ocxz", ops_x, wide, precision=precise)
    size = along.size // length_y
    along_rows = along.reshape(size, length_y)
    x_prev = from_prev[slab:].reshape(x_face)
    x_next = from_next[slab:].reshape(x_face)

    def z_message(face, spot):
        face = face_corners(face, x_prev, x_next, spot)
        return jnp.concatenate([along_rows, face.reshape(3 * length_x, length_y)], axis=0)

    z_prev = shifted(z_message(z_high, slice(-1, None)), "span", 1)
    z_next = shifted(z_message(z_low, slice(0, 1)), "span", -1)
    wide = jnp.concatenate(
        [z_prev[:size].reshape(along.shape), along, z_next[:size].reshape(along.shape)], axis=3
    )
    around = (from_prev, from_next, z_prev, z_next)
    both = jnp.einsum("ocxs,pzs->opcxz", wide, ops_z, precision=precise)
    walls = jnp.concatenate(
        [both[0, 0], both[1, 1], viscosity * (both[2, 1] + both[1, 2])], axis=0
    ).reshape(12, plane)

    u0, u1, t1, *faces, sums_1 = call(
        next_kernel, [shape, shape, *halo, (16, length_y)],
        velocity_old, walls, t0, *around, *tables,
    )
    u2, moments = call(
        last_kernel, [shape, (devices, 18)], t1, *exchange(*faces), *tables, sums_1
    )
    moments = lax.all_to_all(moments, ("wall", "span"), 0, 0, tiled=True)
    (answer,) = call(combine_kernel, [shape], moments, u0, u1, u2)
    return (answer, neumann)


def solution(mesh):
    placed = (
        P(None, "wall", "span", None),
        P(),
        P(("wall", "span"), None),
        P(("wall", "span"), None),
        P(None, ("wall", "span")),
        P(("wall", "span")),
    )
    return jax.shard_map(
        body,
        mesh=mesh,
        in_specs=placed,
        out_specs=(P(None, "wall", "span", None), P(None, ("wall", "span"))),
        check_vma=False,
    )
```
